256 devices in a mesh: group: 8 (over y, core), dev: 32 (over x, z).
Axes of the slice: x: 4, y: 4, z: 8, core: 2. Of those that a mesh axis runs over, the one named last changes fastest.
Arguments:
- tiles: float32 [524288, 3, 128], P(('group', 'dev')), may hold values from -6 to 6
- levels: int32 [524288], P(('group', 'dev')), may hold values from 0 to 2
- new_owner: int32 [524288], P(('group', 'dev')), may hold values from 0 to 31, as said below
- new_slot: int32 [524288], P(('group', 'dev')), may hold values from 0 to 2047
- flags: int32 [524288], P(('group', 'dev')), may hold values 0 or 1
- halo_source: int32 [256, 2, 64], P(('group', 'dev')), may hold values from 0 to 2047
- halo_target: int32 [256, 2, 64], P(('group', 'dev')), may hold values from 0 to 2047
- halo_count: int32 [256, 2], P(('group', 'dev')), may hold values from 1 to 64, as said below
- stiffness: float32 [3, 384, 384], replicated, may hold values from -0.3125 to 0.3125
- nitsche: float32 [384, 384], replicated, may hold values from -0.3125 to 0.3125
- coupling: float32 [384, 384], replicated, may hold values from -0.3125 to 0.3125
Outputs:
- first: float32 [524288, 3, 128], P(('group', 'dev'))
- second: float32 [524288, 3, 128], P(('group', 'dev'))
The draws below stay inside these ranges and needn't reach their ends.
Inputs may be any that keep to these rules, and one draw needn't show every extreme that they name: Within each group, new_owner and new_slot place the group's tiles one to one on its devices' 2048 positions; each device sends at most 80 tiles to one device of its group, and some send exactly 80. `halo_count`: some device's list in each direction holds 64 entries.
All inputs are finite; a program needn't handle non-finite values. No bound on the sum of `flags` on one device may be relied on, other than what follows from the above.
Results may differ from the reference program's by a relative error of at most 0.0001.
Values sent between devices are 32-bit elements; how exact they have to be, the bound alone decides.
A program may use at most 128 MiB of HBM per device.

```python
import jax
import jax.numpy as jnp
from jax import lax

PTS = 128
LEVELS = 3
TILE_DEV = 2048
HALO = 64
TILES = 524288
CAP = 80
N_GROUP = 8
N_DEV = 32
DEVICES = 256


def migration_plan(key):
    base = jax.random.fold_in(key, 11)
    key_a, key_b, key_p, key_q = jax.random.split(base, 4)
    step_size = TILE_DEV // N_DEV
    delta = CAP - step_size
    shift_a = jax.random.randint(key_a, (), 0, N_DEV)
    shift_b = (shift_a + 1 + jax.random.randint(key_b, (), 0, N_DEV - 1)) % N_DEV
    sources = jnp.arange(N_DEV, dtype=jnp.int32)[:, None]
    dests = jnp.arange(N_DEV, dtype=jnp.int32)[None, :]
    offset_gap = (dests - sources) % N_DEV
    counts = step_size + delta * (offset_gap == shift_a).astype(jnp.int32) - delta * (offset_gap == shift_b).astype(jnp.int32)
    ends = jnp.cumsum(counts, axis=1)
    starts = ends - counts
    offsets = jnp.cumsum(counts, axis=0) - counts
    order_keys = jax.random.split(key_p, N_GROUP * N_DEV)
    ranks = jax.vmap(lambda k: jax.random.permutation(k, TILE_DEV))(order_keys).reshape(N_GROUP, N_DEV, TILE_DEV).astype(jnp.int32)
    owner = jnp.sum((ranks[..., None] >= ends[None, :, None, :]).astype(jnp.int32), axis=-1)
    onehot = (owner[..., None] == jnp.arange(N_DEV, dtype=jnp.int32)).astype(jnp.int32)
    within = ranks - jnp.sum(onehot * starts[None, :, None, :], axis=-1)
    place = jnp.sum(onehot * offsets[None, :, None, :], axis=-1) + within
    slot_keys = jax.random.split(key_q, N_GROUP * N_DEV)
    slot_perm = jax.vmap(lambda k: jax.random.permutation(k, TILE_DEV))(slot_keys).reshape(-1).astype(jnp.int32)
    group_ids = jnp.arange(N_GROUP, dtype=jnp.int32)[:, None, None]
    slot = slot_perm[(group_ids * N_DEV + owner) * TILE_DEV + place]
    return (owner.reshape(-1).astype(jnp.int32), slot.reshape(-1).astype(jnp.int32))


def draw_new_owner(key, part):
    return migration_plan(key)[0]


def draw_new_slot(key, part):
    return migration_plan(key)[1]


def halo_plan(key):
    key_s, key_t, key_c, key_f = jax.random.split(jax.random.fold_in(key, 23), 4)
    near = max(TILE_DEV // 4, 1)
    raw_source = jax.random.randint(key_s, (DEVICES, 2, HALO), 0, near)
    source = jnp.stack([raw_source[:, 0, :], TILE_DEV - 1 - raw_source[:, 1, :]], axis=1)
    raw_target = jax.random.randint(key_t, (DEVICES, 2, HALO), 0, near)
    target = jnp.stack([raw_target[:, 0, :], TILE_DEV - 1 - raw_target[:, 1, :]], axis=1)
    counts = jax.random.randint(key_c, (DEVICES, 2), max(HALO // 4, 1), HALO + 1)
    fullest = jax.random.randint(key_f, (2,), 1, DEVICES - 1)
    counts = counts.at[fullest[0], 0].set(HALO).at[fullest[1], 1].set(HALO)
    return (source.astype(jnp.int32), target.astype(jnp.int32), counts.astype(jnp.int32))


def draw_halo_source(key, part):
    return halo_plan(key)[0]


def draw_halo_target(key, part):
    return halo_plan(key)[1]


def draw_halo_count(key, part):
    return halo_plan(key)[2]


def with_ends(entries, stream_key, smallest, largest):
    longest = entries.shape.index(max(entries.shape))
    spots = []
    for shift in (0, 1):
        where = [jax.random.randint(jax.random.fold_in(stream_key, axis), (), 0, length) for axis, length in enumerate(entries.shape)]
        where[longest] = (where[longest] + shift) % entries.shape[longest]
        spots.append(tuple(where))
    return entries.at[spots[0]].set(smallest).at[spots[1]].set(largest)


def block_levels(key, shape, shards, least, top_value):
    gain = 1.0
    for dim, shards_of in shards:
        draws = jax.random.uniform(jax.random.fold_in(jax.random.fold_in(key, 6), dim), (shards_of,), jnp.float32, least / len(shards), top_value / len(shards))
        gain = gain * jnp.repeat(jnp.exp(draws), shape[dim] // shards_of).reshape((-1,) + (1,) * (len(shape) - 1 - dim))
    return gain


def scatter_about(stream_key, shape, deviation, bound, shards=(), kind=jnp.bfloat16):
    gain = block_levels(stream_key, shape, shards, -0.22, 0.18) if shards else 1.0
    entries = jax.random.normal(stream_key, shape, jnp.float32) * deviation * gain
    return jnp.minimum(jnp.maximum(entries, -bound), bound).astype(kind)


def setup_inputs(seed: int = 0) -> dict:
    splits = jax.random.split(jax.random.key(seed), 12)
    return {
        "tiles": scatter_about(splits[0], (TILES, 3, PTS), 1.0, 6.0, ((0, 256),), jnp.float32),
        "levels": with_ends(jax.random.randint(splits[1], (TILES,), 0, LEVELS), jax.random.fold_in(splits[1], 1), 0, LEVELS - 1).astype(jnp.int32),
        "new_owner": draw_new_owner(jax.random.fold_in(splits[11], 71), 0),
        "new_slot": draw_new_slot(jax.random.fold_in(splits[11], 71), 0),
        "flags": with_ends((jax.random.randint(splits[4], (TILES,), 0, 3) < 1).astype(jnp.int32), jax.random.fold_in(splits[4], 1), 0, 1),
        "halo_source": draw_halo_source(jax.random.fold_in(splits[11], 71), 0),
        "halo_target": draw_halo_target(jax.random.fold_in(splits[11], 71), 0),
        "halo_count": draw_halo_count(jax.random.fold_in(splits[11], 71), 0),
        "stiffness": scatter_about(splits[8], (LEVELS, 3 * PTS, 3 * PTS), (3 * PTS) ** -0.5, 0.3125, (), jnp.float32),
        "nitsche": scatter_about(splits[9], (3 * PTS, 3 * PTS), (3 * PTS) ** -0.5, 0.3125, (), jnp.float32),
        "coupling": scatter_about(splits[10], (3 * PTS, 3 * PTS), (3 * PTS) ** -0.5, 0.3125, (), jnp.float32),
    }


def halo_maps(halo_source, halo_target, halo_count):
    dev_ids = jnp.arange(DEVICES, dtype=jnp.int32)[:, None]
    live = jnp.arange(HALO, dtype=jnp.int32)[None, None, :] < halo_count[:, :, None]
    src_next = dev_ids * TILE_DEV + halo_source[:, 1, :]
    dst_next = (dev_ids + 1) * TILE_DEV + jnp.roll(halo_target[:, 0, :], -1, axis=0)
    valid_next = live[:, 1, :] & (dev_ids < DEVICES - 1)
    src_prev = dev_ids * TILE_DEV + halo_source[:, 0, :]
    dst_prev = (dev_ids - 1) * TILE_DEV + jnp.roll(halo_target[:, 1, :], 1, axis=0)
    valid_prev = live[:, 0, :] & (dev_ids >= 1)
    source = jnp.concatenate([src_next.reshape(-1), src_prev.reshape(-1)])
    target = jnp.concatenate([dst_next.reshape(-1), dst_prev.reshape(-1)])
    valid = jnp.concatenate([valid_next.reshape(-1), valid_prev.reshape(-1)])
    return source, jnp.where(valid, target, 0).astype(jnp.int32), valid


def operator(field, level, flags, stiffness, nitsche, coupling, source, target, valid):
    width = field.shape[1]
    result = jnp.zeros_like(field)
    for index in range(LEVELS):
        term = jnp.dot(field, stiffness[index], precision=lax.Precision.HIGHEST)
        result = result + jnp.where((level == index)[:, None], term, 0.0)
    result = result + flags.astype(jnp.float32)[:, None] * jnp.dot(field, nitsche, precision=lax.Precision.HIGHEST)
    position = jnp.arange(field.shape[0], dtype=jnp.int32) % TILE_DEV
    zero_row = jnp.zeros((1, width), jnp.float32)
    before = jnp.concatenate([zero_row, field[:-1]]) * (position != 0)[:, None]
    after = jnp.concatenate([field[1:], zero_row]) * (position != TILE_DEV - 1)[:, None]
    result = result + jnp.dot(before + after, coupling, precision=lax.Precision.HIGHEST)
    rows = field[source] * valid[:, None].astype(jnp.float32)
    images = jnp.dot(rows, coupling, precision=lax.Precision.HIGHEST)
    return result.at[target].add(images)


def reference(tiles, levels, new_owner, new_slot, flags, halo_source, halo_target, halo_count, stiffness, nitsche, coupling):
    total = tiles.shape[0]
    width = tiles.shape[1] * tiles.shape[2]
    flat = tiles.reshape(total, width)
    group_ids = jnp.arange(total, dtype=jnp.int32) // (TILE_DEV * N_DEV)
    dest = ((group_ids * N_DEV + new_owner) * TILE_DEV + new_slot).astype(jnp.int32)
    field = jnp.zeros((total, width), jnp.float32).at[dest].set(flat)
    level = jnp.zeros((total,), jnp.int32).at[dest].set(levels)
    source, target, valid = halo_maps(halo_source, halo_target, halo_count)
    first = operator(field, level, flags, stiffness, nitsche, coupling, source, target, valid)
    second = operator(first, level, flags, stiffness, nitsche, coupling, source, target, valid)
    return first.reshape(tiles.shape), second.reshape(tiles.shape)
```

```python
import functools

import jax
import jax.numpy as jnp
from jax import lax
from jax.experimental import pallas as pl
from jax.experimental.pallas import tpu as pltpu
from jax.sharding import PartitionSpec as P

MESH = pl.DeviceIdType.MESH
LANES = 128
PAD = 8
ROWS = 256
NZ = 8
VMEM_LIMIT = 56 << 20
F32, BF16, I32 = jnp.float32, jnp.bfloat16, jnp.int32


def vmem():
    return pl.BlockSpec(memory_space=pltpu.VMEM)


def smem():
    return pl.BlockSpec(memory_space=pltpu.SMEM)


def hbm():
    return pl.BlockSpec(memory_space=pl.ANY)


def iota(shape, axis):
    return lax.broadcasted_iota(I32, shape, axis)


def nt_dot(a, b):
    return lax.dot_general(a, b, (((1,), (1,)), ((), ())), preferred_element_type=F32)


def dot(a, b):
    return jnp.dot(a, b, preferred_element_type=F32)


def halves(value):
    high = value.astype(BF16)
    return high, (value - high.astype(F32)).astype(BF16)


def plan_kernel(ndev, owner_ref, slot_ref, level_ref, source_ref, meta_ref):
    blocks = owner_ref.shape[0]
    before = (iota((LANES, LANES), 0) < iota((LANES, LANES), 1)).astype(F32).astype(BF16)
    running = jnp.zeros((ndev, 1), F32)
    source = jnp.zeros((2 * ndev, LANES), F32)
    meta = jnp.zeros((8 * ndev, LANES), F32)
    kind = iota((8 * ndev, LANES), 0) % 8
    dest8 = iota((8 * ndev, LANES), 0) // 8
    dest = iota((ndev, LANES), 0)
    for b in range(blocks):
        owner = owner_ref[b : b + 1, :]
        mine = (owner == dest).astype(F32)
        earlier = dot(mine.astype(BF16), before) + running
        running = running + jnp.sum(mine, axis=1, keepdims=True)
        rank = jnp.sum(mine * earlier, axis=0, keepdims=True).astype(I32)
        place = (rank == iota((LANES, LANES), 0)).astype(F32).astype(BF16)
        lane = iota((1, LANES), 1).astype(F32)
        source = source + nt_dot(
            jnp.concatenate([mine * float(b), mine * lane], axis=0).astype(BF16), place
        )
        slot = slot_ref[b : b + 1, :]
        high = (slot // LANES + 1).astype(F32)
        low = (slot % LANES).astype(F32)
        level = level_ref[b : b + 1, :].astype(F32)
        entry = jnp.where(kind == 0, high, jnp.where(kind == 1, low, jnp.where(kind == 2, level, 0.0)))
        entry = jnp.where(owner == dest8, entry, 0.0)
        meta = meta + nt_dot(entry.astype(BF16), place)
    source_ref[...] = (source[:ndev] * float(LANES) + source[ndev:]).astype(I32)
    meta_ref[...] = meta


def exchange_kernel(
    ndev,
    capacity,
    source_ref,
    tiles_ref,
    meta_ref,
    flags_ref,
    stiffness_ref,
    nitsche_ref,
    coupling_ref,
    recv_ref,
    inverse_ref,
    masks_ref,
    weights_ref,
    send_ref,
    meta_recv_ref,
    send_sem,
    recv_sem,
    meta_send_sem,
    meta_recv_sem,
    own_sem,
):
    me = lax.axis_index("dev")
    x, z = me // NZ, me % NZ
    nx = ndev // NZ
    chunk = 3 * capacity

    def offset(step):
        return (11 * step) % ndev

    def peer(off):
        return ((x + off // NZ) % nx) * NZ + (z + off % NZ) % NZ

    def rows_of(off):
        return pl.ds(pl.multiple_of(off * chunk, 8), chunk)

    def meta_copy(step):
        off = offset(step)
        to = peer(off)
        return pltpu.make_async_remote_copy(
            src_ref=meta_ref.at[pl.ds(pl.multiple_of(to * 8, 8), 8)],
            dst_ref=meta_recv_ref.at[pl.ds(pl.multiple_of(off * 8, 8), 8)],
            send_sem=meta_send_sem.at[off],
            recv_sem=meta_recv_sem.at[off],
            device_id={"dev": to},
            device_id_type=MESH,
        )

    def data_copy(step):
        off = offset(step)
        return pltpu.make_async_remote_copy(
            src_ref=send_ref.at[rows_of(off)],
            dst_ref=recv_ref.at[rows_of(off)],
            send_sem=send_sem.at[off],
            recv_sem=recv_sem.at[off],
            device_id={"dev": peer(off)},
            device_id_type=MESH,
        )

    def pack(off):
        to = peer(off)
        base = pl.multiple_of(off * chunk, 8)
        for k in range(capacity):
            row = source_ref[to, k]
            for p in range(3):
                send_ref[pl.ds(base + (p * capacity + k), 1), :] = tiles_ref[p, pl.ds(row, 1), :]

    barrier = pltpu.get_barrier_semaphore()

    @pl.loop(1, ndev)
    def _(step):
        pl.semaphore_signal(
            barrier, inc=1, device_id={"dev": peer(offset(step))}, device_id_type=MESH
        )

    pl.semaphore_wait(barrier, ndev - 1)

    @pl.loop(1, ndev)
    def _(step):
        meta_copy(step).start()

    @pl.loop(1, ndev)
    def _(step):
        pack(offset(step))

        @pl.when(step > 1)
        def _():
            data_copy(step - 1).start()

    pack(0)
    data_copy(ndev - 1).start()
    own_rows = pltpu.make_async_copy(send_ref.at[rows_of(0)], recv_ref.at[rows_of(0)], own_sem.at[0])
    own_meta = pltpu.make_async_copy(
        meta_ref.at[pl.ds(pl.multiple_of(me * 8, 8), 8)], meta_recv_ref.at[pl.ds(0, 8)], own_sem.at[1]
    )
    own_meta.start()

    for group in range(5):
        weight = stiffness_ref[group] if group < 3 else (nitsche_ref, coupling_ref)[group - 3][...]
        high, low = halves(weight)
        weights_ref[pl.ds(group * 384, 384), 0:384] = high
        weights_ref[pl.ds(group * 384, 384), 384:768] = low
    own_rows.start()

    own_meta.wait()

    @pl.loop(1, ndev)
    def _(step):
        meta_copy(step).wait()

    blocks = flags_ref.shape[0]
    kind = iota((3 * blocks, LANES), 0) // blocks
    high_of = iota((3 * blocks, LANES), 0) % blocks + 1
    rank = iota((1, LANES), 1)

    def place(off, total):
        base = pl.multiple_of(off * 8, 8)
        meta = meta_recv_ref[pl.ds(base, 8), :]
        high, low, level = meta[0:1].astype(I32), meta[1:2].astype(I32), meta[2:3]
        value = jnp.where(
            kind == 0,
            jnp.full((1, LANES), off, I32).astype(F32),
            jnp.where(kind == 1, rank.astype(F32), level),
        )
        value = jnp.where(high == high_of, value, 0.0)
        column = (low == iota((LANES, LANES), 0)).astype(F32)
        return total + nt_dot(value.astype(BF16), column.astype(BF16))

    total = lax.fori_loop(0, ndev, place, jnp.zeros((3 * blocks, LANES), F32))
    inverse_ref[...] = (total[:blocks] * float(chunk) + total[blocks : 2 * blocks]).astype(I32)
    level = total[2 * blocks :]
    masks_ref[...] = jnp.concatenate(
        [(level == float(index)).astype(F32) for index in range(3)] + [flags_ref[...].astype(F32)],
        axis=0,
    )

    own_rows.wait()

    @pl.loop(1, ndev)
    def _(step):
        data_copy(step).wait()


def gather_kernel(capacity, inverse_ref, recv_ref, field_ref):
    blocks = inverse_ref.shape[0]
    count = blocks * LANES
    for p in range(3):
        field_ref[p, 0:PAD, :] = jnp.zeros((PAD, LANES), F32)
        field_ref[p, PAD + count : 2 * PAD + count, :] = jnp.zeros((PAD, LANES), F32)

    @pl.loop(0, blocks)
    def _(block):
        base = pl.multiple_of(block * LANES, 8)
        for k in range(LANES):
            row = inverse_ref[block, k]
            for p in range(3):
                field_ref[p, pl.ds(base + (PAD + k), 1), :] = recv_ref[pl.ds(row + p * capacity, 1), :]


def operator_block(field_ref, masks_ref, weights_ref, block):
    base = pl.multiple_of(block * ROWS, ROWS)
    columns = masks_ref[pl.ds(pl.multiple_of(block * ROWS, ROWS), ROWS), :]
    masks = [columns[:, l : l + 1].astype(BF16) for l in range(4)]
    high, low, beside_high, beside_low = [], [], [], []
    for p in range(3):
        wide = field_ref[p, pl.ds(base, ROWS + 2 * PAD), :]
        h, l = halves(wide[PAD : PAD + ROWS])
        high.append(h)
        low.append(l)
        h, l = halves(wide[PAD - 1 : PAD - 1 + ROWS] + wide[PAD + 1 : PAD + 1 + ROWS])
        beside_high.append(h)
        beside_low.append(l)
    left = jnp.concatenate([h * m for m in masks for h in high] + beside_high, axis=1)
    result = dot(left, weights_ref[...])
    left = jnp.concatenate([l * m for m in masks for l in low] + beside_low, axis=1)
    return result[:, :384] + result[:, 384:] + dot(left, weights_ref[:, 0:384])


def halo_images(arrived_ref, weights_ref, images_ref, has_prev, has_next, halo):
    rows = []
    for side, alive in ((0, has_prev), (1, has_next)):
        row = jnp.concatenate(
            [arrived_ref[side, pl.ds(p * halo, halo), :] for p in range(3)], axis=1
        )
        rows.append(jnp.where(alive, row, 0.0))
    high, low = halves(jnp.concatenate(rows, axis=0))
    result = dot(high, weights_ref[1536:1920, :])
    images = result[:, :384] + result[:, 384:] + dot(low, weights_ref[1536:1920, 0:384])
    high, low = halves(images)
    images_ref[0 : 2 * halo, :] = high
    images_ref[2 * halo : 4 * halo, :] = low


def halo_block(target_ref, images_ref, block):
    halo2 = target_ref.shape[1]
    rows = iota((ROWS, halo2), 0) + block * ROWS
    chosen = (rows == target_ref[...]).astype(F32).astype(BF16)
    return dot(jnp.concatenate([chosen, chosen], axis=1), images_ref[...])


def neighbours(groups, ndev):
    group, dev = lax.axis_index("group"), lax.axis_index("dev")
    me = group * ndev + dev
    total = groups * ndev
    after, prior = (me + 1) % total, (me + total - 1) % total
    return me, (prior // ndev, prior % ndev), (after // ndev, after % ndev)


def first_kernel(
    groups,
    ndev,
    source_ref,
    count_ref,
    field_ref,
    masks_ref,
    weights_ref,
    target_ref,
    first_ref,
    second_halo_ref,
    send_ref,
    arrived_ref,
    arrived2_ref,
    images_ref,
    send_sem,
    recv_sem,
):
    halo = source_ref.shape[1]
    blocks = (field_ref.shape[1] - 2 * PAD) // ROWS
    me, prior, after = neighbours(groups, ndev)
    has_prev, has_next = me > 0, me < groups * ndev - 1

    barrier = pltpu.get_barrier_semaphore()
    for other in (prior, after):
        pl.semaphore_signal(barrier, inc=1, device_id=other, device_id_type=MESH)
    pl.semaphore_wait(barrier, 2)

    def copies(turn, into):
        return [
            pltpu.make_async_remote_copy(
                src_ref=send_ref.at[turn, side],
                dst_ref=into.at[1 - side],
                send_sem=send_sem.at[turn, side],
                recv_sem=recv_sem.at[turn, side],
                device_id=(prior, after)[side],
                device_id_type=MESH,
            )
            for side in range(2)
        ]

    def pack(turn, rows_ref):
        for side in range(2):
            for k in range(halo):
                row = source_ref[side, k] + PAD
                for p in range(3):
                    send_ref[turn, side, pl.ds(p * halo + k, 1), :] = rows_ref[p, pl.ds(row, 1), :]
            live = iota((halo, LANES), 0) < count_ref[0, side]
            for p in range(3):
                part = pl.ds(p * halo, halo)
                send_ref[turn, side, part, :] = jnp.where(live, send_ref[turn, side, part, :], 0.0)

    def local(block):
        result = operator_block(field_ref, masks_ref, weights_ref, block)
        rows = pl.ds(pl.multiple_of(block * ROWS, ROWS) + PAD, ROWS)
        for p in range(3):
            first_ref[p, rows, :] = result[:, p * LANES : (p + 1) * LANES]

    pack(0, field_ref)
    for p in range(3):
        first_ref[p, 0:PAD, :] = jnp.zeros((PAD, LANES), F32)
        first_ref[p, PAD + blocks * ROWS : 2 * PAD + blocks * ROWS, :] = jnp.zeros((PAD, LANES), F32)
    local(0)
    sent = copies(0, arrived_ref)
    for copy in sent:
        copy.start()

    @pl.loop(1, blocks)
    def _(block):
        local(block)

    for copy in sent:
        copy.wait()
    halo_images(arrived_ref, weights_ref, images_ref, has_prev, has_next, halo)

    @pl.loop(0, blocks)
    def _(block):
        added = halo_block(target_ref, images_ref, block)
        rows = pl.ds(pl.multiple_of(block * ROWS, ROWS) + PAD, ROWS)
        for p in range(3):
            first_ref[p, rows, :] = first_ref[p, rows, :] + added[:, p * LANES : (p + 1) * LANES]

    pack(1, first_ref)
    sent = copies(1, arrived2_ref)
    for copy in sent:
        copy.start()
    for copy in sent:
        copy.wait()
    second_halo_ref[...] = arrived2_ref[...]


def second_kernel(
    groups,
    ndev,
    field_ref,
    masks_ref,
    weights_ref,
    target_ref,
    arrived_ref,
    first_ref,
    second_ref,
    images_ref,
):
    halo = arrived_ref.shape[1] // 3
    block = pl.program_id(0)

    @pl.when(block == 0)
    def _():
        me, _, _ = neighbours(groups, ndev)
        halo_images(arrived_ref, weights_ref, images_ref, me > 0, me < groups * ndev - 1, halo)

    result = operator_block(field_ref, masks_ref, weights_ref, block)
    result = result + halo_block(target_ref, images_ref, block)
    rows = pl.ds(pl.multiple_of(block * ROWS, ROWS) + PAD, ROWS)
    for p in range(3):
        first_ref[p] = field_ref[p, rows, :]
        second_ref[p] = result[:, p * LANES : (p + 1) * LANES]


def local(
    groups,
    ndev,
    tiles,
    levels,
    new_owner,
    new_slot,
    flags,
    halo_source,
    halo_target,
    halo_count,
    stiffness,
    nitsche,
    coupling,
):
    count = tiles.shape[0]
    halo = halo_source.shape[2]
    blocks = count // LANES
    capacity = count // ndev + count // (4 * ndev)
    planes = jnp.transpose(tiles, (1, 0, 2))
    by_lane = (blocks, LANES)
    shape = jax.ShapeDtypeStruct

    source, meta = pl.pallas_call(
        functools.partial(plan_kernel, ndev),
        out_shape=(shape((ndev, LANES), I32), shape((8 * ndev, LANES), F32)),
        in_specs=[vmem()] * 3,
        out_specs=(vmem(), vmem()),
        name="plan",
    )(new_owner.reshape(by_lane), new_slot.reshape(by_lane), levels.reshape(by_lane))

    arrivals = ndev * 3 * capacity
    recv, inverse, masks, weights = pl.pallas_call(
        functools.partial(exchange_kernel, ndev, capacity),
        out_shape=(
            shape((arrivals, LANES), F32),
            shape(by_lane, I32),
            shape((4 * blocks, LANES), F32),
            shape((1920, 768), BF16),
        ),
        in_specs=[smem()] + [vmem()] * 6,
        out_specs=(hbm(), vmem(), vmem(), vmem()),
        scratch_shapes=[
            pltpu.VMEM((arrivals, LANES), F32),
            pltpu.VMEM((8 * ndev, LANES), F32),
            pltpu.SemaphoreType.DMA((ndev,)),
            pltpu.SemaphoreType.DMA((ndev,)),
            pltpu.SemaphoreType.DMA((ndev,)),
            pltpu.SemaphoreType.DMA((ndev,)),
            pltpu.SemaphoreType.DMA((2,)),
        ],
        compiler_params=pltpu.CompilerParams(
            collective_id=0, has_side_effects=True, vmem_limit_bytes=VMEM_LIMIT
        ),
        name="exchange",
    )(source, planes, meta, flags.reshape(by_lane), stiffness, nitsche, coupling)

    field = pl.pallas_call(
        functools.partial(gather_kernel, capacity),
        out_shape=shape((3, count + 2 * PAD, LANES), F32),
        in_specs=[smem(), vmem()],
        out_specs=vmem(),
        compiler_params=pltpu.CompilerParams(vmem_limit_bytes=VMEM_LIMIT),
        name="gather",
    )(inverse, recv)

    masks = masks.reshape(4, count).T
    targets = halo_target.reshape(1, 2 * halo)
    first, second_halo = pl.pallas_call(
        functools.partial(first_kernel, groups, ndev),
        out_shape=(shape(field.shape, F32), shape((2, 3 * halo, LANES), F32)),
        in_specs=[smem(), smem()] + [vmem()] * 4,
        out_specs=(vmem(), vmem()),
        scratch_shapes=[
            pltpu.VMEM((2, 2, 3 * halo, LANES), F32),
            pltpu.VMEM((2, 3 * halo, LANES), F32),
            pltpu.VMEM((2, 3 * halo, LANES), F32),
            pltpu.VMEM((4 * halo, 384), BF16),
            pltpu.SemaphoreType.DMA((2, 2)),
            pltpu.SemaphoreType.DMA((2, 2)),
        ],
        compiler_params=pltpu.CompilerParams(
            collective_id=1, has_side_effects=True, vmem_limit_bytes=VMEM_LIMIT
        ),
        name="first",
    )(halo_source[0], halo_count, field, masks, weights, targets)

    block = pl.BlockSpec((3, ROWS, LANES), lambda b: (0, b, 0))
    first, second = pl.pallas_call(
        functools.partial(second_kernel, groups, ndev),
        grid=(count // ROWS,),
        out_shape=(shape(planes.shape, F32), shape(planes.shape, F32)),
        in_specs=[vmem()] * 5,
        out_specs=(block, block),
        scratch_shapes=[pltpu.VMEM((4 * halo, 384), BF16)],
        compiler_params=pltpu.CompilerParams(vmem_limit_bytes=VMEM_LIMIT),
        name="second",
    )(first, masks, weights, targets, second_halo)
    return jnp.transpose(first, (1, 0, 2)), jnp.transpose(second, (1, 0, 2))


def solution(mesh):
    whole = P(("group", "dev"))
    return jax.shard_map(
        functools.partial(local, mesh.shape["group"], mesh.shape["dev"]),
        mesh=mesh,
        in_specs=(
            P(("group", "dev"), None, None),
            whole,
            whole,
            whole,
            whole,
            P(("group", "dev"), None, None),
            P(("group", "dev"), None, None),
            P(("group", "dev"), None),
            P(),
            P(),
            P(),
        ),
        out_specs=(P(("group", "dev"), None, None), P(("group", "dev"), None, None)),
        check_vma=False,
    )
```

```python
import functools

import jax
import jax.numpy as jnp
from jax import lax
from jax.experimental import pallas as pl
from jax.experimental.pallas import tpu as pltpu
from jax.sharding import PartitionSpec as P

MESH = pl.DeviceIdType.MESH
LANES = 128
PAD = 8
ROWS = 256
NZ = 8
VMEM_LIMIT = 56 << 20
F32, BF16, I32 = jnp.float32, jnp.bfloat16, jnp.int32


def vmem():
    return pl.BlockSpec(memory_space=pltpu.VMEM)


def smem():
    return pl.BlockSpec(memory_space=pltpu.SMEM)


def hbm():
    return pl.BlockSpec(memory_space=pl.ANY)


def iota(shape, axis):
    return lax.broadcasted_iota(I32, shape, axis)


def nt_dot(a, b):
    return lax.dot_general(a, b, (((1,), (1,)), ((), ())), preferred_element_type=F32)


def dot(a, b):
    return jnp.dot(a, b, preferred_element_type=F32)


def halves(value):
    high = value.astype(BF16)
    return high, (value - high.astype(F32)).astype(BF16)


def plan_kernel(ndev, owner_ref, slot_ref, level_ref, source_ref, meta_ref):
    blocks = owner_ref.shape[0]
    before = (iota((LANES, LANES), 0) < iota((LANES, LANES), 1)).astype(F32).astype(BF16)
    running = jnp.zeros((ndev, 1), F32)
    source = jnp.zeros((2 * ndev, LANES), F32)
    meta = jnp.zeros((8 * ndev, LANES), F32)
    kind = iota((8 * ndev, LANES), 0) % 8
    dest8 = iota((8 * ndev, LANES), 0) // 8
    dest = iota((ndev, LANES), 0)
    for b in range(blocks):
        owner = owner_ref[b : b + 1, :]
        mine = (owner == dest).astype(F32)
        earlier = dot(mine.astype(BF16), before) + running
        running = running + jnp.sum(mine, axis=1, keepdims=True)
        rank = jnp.sum(mine * earlier, axis=0, keepdims=True).astype(I32)
        place = (rank == iota((LANES, LANES), 0)).astype(F32).astype(BF16)
        lane = iota((1, LANES), 1).astype(F32)
        source = source + nt_dot(
            jnp.concatenate([mine * float(b), mine * lane], axis=0).astype(BF16), place
        )
        slot = slot_ref[b : b + 1, :]
        high = (slot // LANES + 1).astype(F32)
        low = (slot % LANES).astype(F32)
        level = level_ref[b : b + 1, :].astype(F32)
        entry = jnp.where(kind == 0, high, jnp.where(kind == 1, low, jnp.where(kind == 2, level, 0.0)))
        entry = jnp.where(owner == dest8, entry, 0.0)
        meta = meta + nt_dot(entry.astype(BF16), place)
    source_ref[...] = (source[:ndev] * float(LANES) + source[ndev:]).astype(I32)
    meta_ref[...] = meta


def exchange_kernel(
    groups,
    ndev,
    capacity,
    source_ref,
    halo_source_ref,
    count_ref,
    tiles_ref,
    meta_ref,
    flags_ref,
    stiffness_ref,
    nitsche_ref,
    coupling_ref,
    target_ref,
    first_ref,
    masks_ref,
    weights_ref,
    second_halo_ref,
    send_ref,
    recv_ref,
    meta_recv_ref,
    arrival_masks_ref,
    own_ref,
    near_ref,
    sums_ref,
    inverse_ref,
    inverse_smem,
    halo_send_ref,
    arrived_ref,
    arrived2_ref,
    images_ref,
    send_sem,
    recv_sem,
    meta_send_sem,
    meta_recv_sem,
    own_sem,
    halo_send_sem,
    halo_recv_sem,
):
    me = lax.axis_index("dev")
    x, z = me // NZ, me % NZ
    nx = ndev // NZ
    chunk = 3 * capacity
    halo = halo_source_ref.shape[1]
    count = first_ref.shape[1] - 2 * PAD
    curve, prior, after = neighbours(groups, ndev)
    has_prev, has_next = curve > 0, curve < groups * ndev - 1

    def offset(step):
        return (11 * step) % ndev

    def peer(off):
        return ((x + off // NZ) % nx) * NZ + (z + off % NZ) % NZ

    def rows_of(off):
        return pl.ds(pl.multiple_of(off * chunk, 8), chunk)

    def meta_copy(step):
        off = offset(step)
        to = peer(off)
        return pltpu.make_async_remote_copy(
            src_ref=meta_ref.at[pl.ds(pl.multiple_of(to * 8, 8), 8)],
            dst_ref=meta_recv_ref.at[pl.ds(pl.multiple_of(off * 8, 8), 8)],
            send_sem=meta_send_sem.at[off],
            recv_sem=meta_recv_sem.at[off],
            device_id={"dev": to},
            device_id_type=MESH,
        )

    def data_copy(step):
        off = offset(step)
        return pltpu.make_async_remote_copy(
            src_ref=send_ref.at[rows_of(off)],
            dst_ref=recv_ref.at[rows_of(off)],
            send_sem=send_sem.at[off],
            recv_sem=recv_sem.at[off],
            device_id={"dev": peer(off)},
            device_id_type=MESH,
        )

    def halo_copies(turn, into):
        return [
            pltpu.make_async_remote_copy(
                src_ref=halo_send_ref.at[turn, side],
                dst_ref=into.at[1 - side, pl.ds(0, 3 * halo)],
                send_sem=halo_send_sem.at[turn, side],
                recv_sem=halo_recv_sem.at[turn, side],
                device_id=(prior, after)[side],
                device_id_type=MESH,
            )
            for side in range(2)
        ]

    def pack(off):
        to = peer(off)
        base = pl.multiple_of(off * chunk, 8)
        for k in range(capacity):
            row = source_ref[to, k]
            for p in range(3):
                send_ref[pl.ds(base + (p * capacity + k), 1), :] = tiles_ref[p, pl.ds(row, 1), :]

    barrier = pltpu.get_barrier_semaphore()

    @pl.loop(1, ndev)
    def _(step):
        pl.semaphore_signal(
            barrier, inc=1, device_id={"dev": peer(offset(step))}, device_id_type=MESH
        )

    for other in (prior, after):
        pl.semaphore_signal(barrier, inc=1, device_id=other, device_id_type=MESH)
    pl.semaphore_wait(barrier, ndev + 1)

    @pl.loop(1, ndev)
    def _(step):
        meta_copy(step).start()

    @pl.loop(1, ndev)
    def _(step):
        pack(offset(step))

        @pl.when(step > 1)
        def _():
            data_copy(step - 1).start()

    pack(0)
    data_copy(ndev - 1).start()
    own_rows = pltpu.make_async_copy(send_ref.at[rows_of(0)], recv_ref.at[rows_of(0)], own_sem.at[0])
    own_meta = pltpu.make_async_copy(
        meta_ref.at[pl.ds(pl.multiple_of(me * 8, 8), 8)], meta_recv_ref.at[pl.ds(0, 8)], own_sem.at[1]
    )
    own_meta.start()

    for group in range(5):
        weight = stiffness_ref[group] if group < 3 else (nitsche_ref, coupling_ref)[group - 3][...]
        high, low = halves(weight)
        weights_ref[pl.ds(group * 384, 384), 0:384] = high
        weights_ref[pl.ds(group * 384, 384), 384:768] = low
    own_rows.start()

    own_meta.wait()

    @pl.loop(1, ndev)
    def _(step):
        meta_copy(step).wait()

    blocks = flags_ref.shape[0]
    kind = iota((3 * blocks, LANES), 0) // blocks
    high_of = iota((3 * blocks, LANES), 0) % blocks + 1
    rank = iota((1, LANES), 1)
    flag_bits = flags_ref[...].astype(F32).astype(BF16)
    diagonal = (iota((LANES, LANES), 0) == iota((LANES, LANES), 1)).astype(F32).astype(BF16)
    term = iota((8, LANES), 0)

    def place(off, total):
        base = pl.multiple_of(off * 8, 8)
        meta = meta_recv_ref[pl.ds(base, 8), :]
        high, low, level = meta[0:1].astype(I32), meta[1:2].astype(I32), meta[2:3]
        value = jnp.where(
            kind == 0,
            jnp.full((1, LANES), off, I32).astype(F32),
            jnp.where(kind == 1, rank.astype(F32), level),
        )
        value = jnp.where(high == high_of, value, 0.0)
        column = (low == iota((LANES, LANES), 0)).astype(F32).astype(BF16)
        flag = jnp.where(high == iota((blocks, LANES), 0) + 1, dot(flag_bits, column), 0.0)
        flag = jnp.sum(flag, axis=0, keepdims=True)
        bits = jnp.where(term == 3, flag, (level == term.astype(F32)).astype(F32))
        across = nt_dot(diagonal, bits.astype(BF16))
        arrival_masks_ref[pl.ds(pl.multiple_of(off * capacity, 8), capacity), :] = across[:capacity]
        return total + nt_dot(value.astype(BF16), column)

    total = lax.fori_loop(0, ndev, place, jnp.zeros((3 * blocks, LANES), F32))
    arrival = (total[:blocks] * float(chunk) + total[blocks : 2 * blocks] * 3.0).astype(I32)
    inverse_ref[...] = jnp.clip(arrival, 0, (ndev - 1) * chunk + chunk - 3)
    to_smem = pltpu.make_async_copy(inverse_ref, inverse_smem, own_sem.at[2])
    to_smem.start()
    level = total[2 * blocks :]
    masks_ref[...] = jnp.concatenate(
        [(level == float(index)).astype(F32) for index in range(3)] + [flags_ref[...].astype(F32)],
        axis=0,
    )

    def products(pair):
        offs = [offset(2 * pair + i) for i in range(2)]
        bases = [pl.multiple_of(off * chunk, 8) for off in offs]
        columns = jnp.concatenate(
            [
                arrival_masks_ref[pl.ds(pl.multiple_of(off * capacity, 8), capacity), :]
                for off in offs
            ],
            axis=0,
        )
        masks = [columns[:, l : l + 1].astype(BF16) for l in range(4)]
        high, low = [], []
        for p in range(3):
            h, l = halves(
                jnp.concatenate(
                    [recv_ref[pl.ds(base + p * capacity, capacity), :] for base in bases], axis=0
                )
            )
            high.append(h)
            low.append(l)
        result = dot(jnp.concatenate([h * m for m in masks for h in high], axis=1), weights_ref[0:1536, :])
        own = (
            result[:, :384]
            + result[:, 384:]
            + dot(jnp.concatenate([l * m for m in masks for l in low], axis=1), weights_ref[0:1536, 0:384])
        )
        result = dot(jnp.concatenate(high, axis=1), weights_ref[1536:1920, :])
        near = (
            result[:, :384]
            + result[:, 384:]
            + dot(jnp.concatenate(low, axis=1), weights_ref[1536:1920, 0:384])
        )
        for i, base in enumerate(bases):
            part = slice(i * capacity, (i + 1) * capacity)
            for p in range(3):
                rows = pl.ds(base + p, capacity, stride=3)
                own_ref[rows, :] = own[part, p * LANES : (p + 1) * LANES]
                near_ref[rows, :] = near[part, p * LANES : (p + 1) * LANES]

    own_rows.wait()
    data_copy(1).wait()
    products(0)

    @pl.loop(1, ndev // 2)
    def _(pair):
        data_copy(2 * pair).wait()
        data_copy(2 * pair + 1).wait()
        products(pair)

    def arrival_of(block, lane):
        return jnp.clip(inverse_smem[block, lane], 0, (ndev - 1) * chunk + chunk - 3)

    to_smem.wait()
    for side in range(2):
        for k in range(halo):
            slot = halo_source_ref[side, k]
            row = arrival_of(slot // LANES, slot % LANES)
            halo_send_ref[0, side, pl.ds(3 * k, 3), :] = near_ref[pl.ds(row, 3), :]
        live = iota((3 * halo, LANES), 0) < 3 * count_ref[0, side]
        halo_send_ref[0, side] = jnp.where(live, halo_send_ref[0, side], 0.0)

    def gather(block, carry):
        before, here, row = carry
        base = pl.multiple_of(block * (3 * LANES), 8)
        for k in range(LANES):
            if k < LANES - 1:
                later = arrival_of(block, k + 1)
                ahead = near_ref[pl.ds(later, 3), :]
            else:
                later = arrival_of(jnp.minimum(block + 1, blocks - 1), 0)
                ahead = jnp.where(block < blocks - 1, near_ref[pl.ds(later, 3), :], 0.0)
            sums_ref[pl.ds(base + 3 * k, 3), :] = own_ref[pl.ds(row, 3), :] + (before + ahead)
            before, here, row = here, ahead, later
        return before, here, row

    row = arrival_of(0, 0)
    start = (jnp.zeros((3, LANES), F32), near_ref[pl.ds(row, 3), :], row)
    start = gather(0, start)
    sent = halo_copies(0, arrived_ref)
    for copy in sent:
        copy.start()
    lax.fori_loop(1, blocks, gather, start)
    for p in range(3):
        first_ref[p, 0:PAD, :] = jnp.zeros((PAD, LANES), F32)
        first_ref[p, PAD + count : 2 * PAD + count, :] = jnp.zeros((PAD, LANES), F32)

    for copy in sent:
        copy.wait()
    rows = []
    for side, alive in ((0, has_prev), (1, has_next)):
        row = jnp.concatenate(
            [arrived_ref[side, pl.ds(p, halo, stride=3), :] for p in range(3)], axis=1
        )
        rows.append(jnp.where(alive, row, 0.0))
    high, low = halves(jnp.concatenate(rows, axis=0))
    images_ref[0 : 2 * halo, :] = high
    images_ref[2 * halo : 4 * halo, :] = low

    @pl.loop(0, count // ROWS)
    def _(block):
        added = halo_block(target_ref, images_ref, block)
        base = pl.multiple_of(block * (3 * ROWS), 8)
        rows = pl.ds(pl.multiple_of(block * ROWS, ROWS) + PAD, ROWS)
        for p in range(3):
            first_ref[p, rows, :] = (
                sums_ref[pl.ds(base + p, ROWS, stride=3), :] + added[:, p * LANES : (p + 1) * LANES]
            )

    for side in range(2):
        for k in range(halo):
            row = halo_source_ref[side, k] + PAD
            for p in range(3):
                halo_send_ref[1, side, pl.ds(p * halo + k, 1), :] = first_ref[p, pl.ds(row, 1), :]
        live = iota((halo, LANES), 0) < count_ref[0, side]
        for p in range(3):
            part = pl.ds(p * halo, halo)
            halo_send_ref[1, side, part, :] = jnp.where(live, halo_send_ref[1, side, part, :], 0.0)
    sent = halo_copies(1, arrived2_ref)
    for copy in sent:
        copy.start()
    for copy in sent:
        copy.wait()
    second_halo_ref[...] = arrived2_ref[:, 0 : 3 * halo, :]


def operator_block(field_ref, masks_ref, weights_ref, block):
    base = pl.multiple_of(block * ROWS, ROWS)
    columns = masks_ref[pl.ds(pl.multiple_of(block * ROWS, ROWS), ROWS), :]
    masks = [columns[:, l : l + 1].astype(BF16) for l in range(4)]
    high, low, beside_high, beside_low = [], [], [], []
    for p in range(3):
        wide = field_ref[p, pl.ds(base, ROWS + 2 * PAD), :]
        h, l = halves(wide[PAD : PAD + ROWS])
        high.append(h)
        low.append(l)
        h, l = halves(wide[PAD - 1 : PAD - 1 + ROWS] + wide[PAD + 1 : PAD + 1 + ROWS])
        beside_high.append(h)
        beside_low.append(l)
    left = jnp.concatenate([h * m for m in masks for h in high] + beside_high, axis=1)
    result = dot(left, weights_ref[...])
    left = jnp.concatenate([l * m for m in masks for l in low] + beside_low, axis=1)
    return result[:, :384] + result[:, 384:] + dot(left, weights_ref[:, 0:384])


def halo_images(arrived_ref, weights_ref, images_ref, has_prev, has_next, halo):
    rows = []
    for side, alive in ((0, has_prev), (1, has_next)):
        row = jnp.concatenate(
            [arrived_ref[side, pl.ds(p * halo, halo), :] for p in range(3)], axis=1
        )
        rows.append(jnp.where(alive, row, 0.0))
    high, low = halves(jnp.concatenate(rows, axis=0))
    result = dot(high, weights_ref[1536:1920, :])
    images = result[:, :384] + result[:, 384:] + dot(low, weights_ref[1536:1920, 0:384])
    high, low = halves(images)
    images_ref[0 : 2 * halo, :] = high
    images_ref[2 * halo : 4 * halo, :] = low


def halo_block(target_ref, images_ref, block):
    halo2 = target_ref.shape[1]
    rows = iota((ROWS, halo2), 0) + block * ROWS
    chosen = (rows == target_ref[...]).astype(F32).astype(BF16)
    return dot(jnp.concatenate([chosen, chosen], axis=1), images_ref[...])


def neighbours(groups, ndev):
    group, dev = lax.axis_index("group"), lax.axis_index("dev")
    me = group * ndev + dev
    total = groups * ndev
    after, prior = (me + 1) % total, (me + total - 1) % total
    return me, (prior // ndev, prior % ndev), (after // ndev, after % ndev)


def second_kernel(
    groups,
    ndev,
    field_ref,
    masks_ref,
    weights_ref,
    target_ref,
    arrived_ref,
    first_ref,
    second_ref,
    images_ref,
):
    halo = arrived_ref.shape[1] // 3
    block = pl.program_id(0)

    @pl.when(block == 0)
    def _():
        me, _, _ = neighbours(groups, ndev)
        halo_images(arrived_ref, weights_ref, images_ref, me > 0, me < groups * ndev - 1, halo)

    result = operator_block(field_ref, masks_ref, weights_ref, block)
    result = result + halo_block(target_ref, images_ref, block)
    rows = pl.ds(pl.multiple_of(block * ROWS, ROWS) + PAD, ROWS)
    for p in range(3):
        first_ref[p] = field_ref[p, rows, :]
        second_ref[p] = result[:, p * LANES : (p + 1) * LANES]


def local(
    groups,
    ndev,
    tiles,
    levels,
    new_owner,
    new_slot,
    flags,
    halo_source,
    halo_target,
    halo_count,
    stiffness,
    nitsche,
    coupling,
):
    count = tiles.shape[0]
    halo = halo_source.shape[2]
    blocks = count // LANES
    capacity = count // ndev + count // (4 * ndev)
    planes = jnp.transpose(tiles, (1, 0, 2))
    by_lane = (blocks, LANES)
    shape = jax.ShapeDtypeStruct

    source, meta = pl.pallas_call(
        functools.partial(plan_kernel, ndev),
        out_shape=(shape((ndev, LANES), I32), shape((8 * ndev, LANES), F32)),
        in_specs=[vmem()] * 3,
        out_specs=(vmem(), vmem()),
        name="plan",
    )(new_owner.reshape(by_lane), new_slot.reshape(by_lane), levels.reshape(by_lane))

    arrivals = ndev * 3 * capacity
    targets = halo_target.reshape(1, 2 * halo)
    first, masks, weights, second_halo = pl.pallas_call(
        functools.partial(exchange_kernel, groups, ndev, capacity),
        out_shape=(
            shape((3, count + 2 * PAD, LANES), F32),
            shape((4 * blocks, LANES), F32),
            shape((1920, 768), BF16),
            shape((2, 3 * halo, LANES), F32),
        ),
        in_specs=[smem()] * 3 + [vmem()] * 7,
        out_specs=(vmem(), vmem(), vmem(), vmem()),
        scratch_shapes=[
            pltpu.VMEM((arrivals, LANES), F32),
            pltpu.VMEM((arrivals, LANES), F32),
            pltpu.VMEM((8 * ndev, LANES), F32),
            pltpu.VMEM((ndev * capacity, 8), F32),
            pltpu.VMEM((arrivals + 8, LANES), F32),
            pltpu.VMEM((arrivals + 8, LANES), F32),
            pltpu.VMEM((3 * count + 8, LANES), F32),
            pltpu.VMEM(by_lane, I32),
            pltpu.SMEM(by_lane, I32),
            pltpu.VMEM((2, 2, 3 * halo, LANES), F32),
            pltpu.VMEM((2, 3 * halo + 8, LANES), F32),
            pltpu.VMEM((2, 3 * halo + 8, LANES), F32),
            pltpu.VMEM((4 * halo, 384), BF16),
            pltpu.SemaphoreType.DMA((ndev,)),
            pltpu.SemaphoreType.DMA((ndev,)),
            pltpu.SemaphoreType.DMA((ndev,)),
            pltpu.SemaphoreType.DMA((ndev,)),
            pltpu.SemaphoreType.DMA((3,)),
            pltpu.SemaphoreType.DMA((2, 2)),
            pltpu.SemaphoreType.DMA((2, 2)),
        ],
        compiler_params=pltpu.CompilerParams(
            collective_id=0, has_side_effects=True, vmem_limit_bytes=VMEM_LIMIT
        ),
        name="exchange",
    )(
        source,
        halo_source[0],
        halo_count,
        planes,
        meta,
        flags.reshape(by_lane),
        stiffness,
        nitsche,
        coupling,
        targets,
    )

    masks = masks.reshape(4, count).T
    block = pl.BlockSpec((3, ROWS, LANES), lambda b: (0, b, 0))
    first, second = pl.pallas_call(
        functools.partial(second_kernel, groups, ndev),
        grid=(count // ROWS,),
        out_shape=(shape(planes.shape, F32), shape(planes.shape, F32)),
        in_specs=[vmem()] * 5,
        out_specs=(block, block),
        scratch_shapes=[pltpu.VMEM((4 * halo, 384), BF16)],
        compiler_params=pltpu.CompilerParams(vmem_limit_bytes=VMEM_LIMIT),
        name="second",
    )(first, masks, weights, targets, second_halo)
    return jnp.transpose(first, (1, 0, 2)), jnp.transpose(second, (1, 0, 2))


def solution(mesh):
    whole = P(("group", "dev"))
    return jax.shard_map(
        functools.partial(local, mesh.shape["group"], mesh.shape["dev"]),
        mesh=mesh,
        in_specs=(
            P(("group", "dev"), None, None),
            whole,
            whole,
            whole,
            whole,
            P(("group", "dev"), None, None),
            P(("group", "dev"), None, None),
            P(("group", "dev"), None),
            P(),
            P(),
            P(),
        ),
        out_specs=(P(("group", "dev"), None, None), P(("group", "dev"), None, None)),
        check_vma=False,
    )
```

```python
import functools

import jax
import jax.numpy as jnp
from jax import lax
from jax.experimental import pallas as pl
from jax.experimental.pallas import tpu as pltpu
from jax.sharding import PartitionSpec as P

MESH = pl.DeviceIdType.MESH
LANES = 128
PAD = 8
ROWS = 256
NZ = 8
VMEM_LIMIT = 56 << 20
F32, BF16, I32 = jnp.float32, jnp.bfloat16, jnp.int32


def vmem():
    return pl.BlockSpec(memory_space=pltpu.VMEM)


def smem():
    return pl.BlockSpec(memory_space=pltpu.SMEM)


def hbm():
    return pl.BlockSpec(memory_space=pl.ANY)


def iota(shape, axis):
    return lax.broadcasted_iota(I32, shape, axis)


def nt_dot(a, b):
    return lax.dot_general(a, b, (((1,), (1,)), ((), ())), preferred_element_type=F32)


def dot(a, b):
    return jnp.dot(a, b, preferred_element_type=F32)


def halves(value):
    high = value.astype(BF16)
    return high, (value - high.astype(F32)).astype(BF16)


def plan_kernel(ndev, owner_ref, slot_ref, level_ref, source_ref, meta_ref):
    blocks = owner_ref.shape[0]
    before = (iota((LANES, LANES), 0) < iota((LANES, LANES), 1)).astype(F32).astype(BF16)
    running = jnp.zeros((ndev, 1), F32)
    source = jnp.zeros((2 * ndev, LANES), F32)
    meta = jnp.zeros((8 * ndev, LANES), F32)
    kind = iota((8 * ndev, LANES), 0) % 8
    dest8 = iota((8 * ndev, LANES), 0) // 8
    dest = iota((ndev, LANES), 0)
    for b in range(blocks):
        owner = owner_ref[b : b + 1, :]
        mine = (owner == dest).astype(F32)
        earlier = dot(mine.astype(BF16), before) + running
        running = running + jnp.sum(mine, axis=1, keepdims=True)
        rank = jnp.sum(mine * earlier, axis=0, keepdims=True).astype(I32)
        place = (rank == iota((LANES, LANES), 0)).astype(F32).astype(BF16)
        lane = iota((1, LANES), 1).astype(F32)
        source = source + nt_dot(
            jnp.concatenate([mine * float(b), mine * lane], axis=0).astype(BF16), place
        )
        slot = slot_ref[b : b + 1, :]
        high = (slot // LANES + 1).astype(F32)
        low = (slot % LANES).astype(F32)
        level = level_ref[b : b + 1, :].astype(F32)
        entry = jnp.where(kind == 0, high, jnp.where(kind == 1, low, jnp.where(kind == 2, level, 0.0)))
        entry = jnp.where(owner == dest8, entry, 0.0)
        meta = meta + nt_dot(entry.astype(BF16), place)
    source_ref[...] = (source[:ndev] * float(LANES) + source[ndev:]).astype(I32)
    meta_ref[...] = meta


def exchange_kernel(
    groups,
    ndev,
    capacity,
    source_ref,
    halo_source_ref,
    count_ref,
    tiles_ref,
    meta_ref,
    flags_ref,
    stiffness_ref,
    nitsche_ref,
    coupling_ref,
    target_ref,
    first_ref,
    masks_ref,
    weights_ref,
    second_halo_ref,
    send_ref,
    recv_ref,
    meta_recv_ref,
    arrival_masks_ref,
    own_ref,
    near_ref,
    sums_ref,
    inverse_ref,
    inverse_smem,
    halo_send_ref,
    arrived_ref,
    arrived2_ref,
    images_ref,
    send_sem,
    recv_sem,
    meta_send_sem,
    meta_recv_sem,
    own_sem,
    halo_send_sem,
    halo_recv_sem,
):
    me = lax.axis_index("dev")
    x, z = me // NZ, me % NZ
    nx = ndev // NZ
    chunk = 3 * capacity
    halo = halo_source_ref.shape[1]
    count = first_ref.shape[1] - 2 * PAD
    curve, prior, after = neighbours(groups, ndev)
    has_prev, has_next = curve > 0, curve < groups * ndev - 1

    def offset(step):
        return (11 * step) % ndev

    def peer(off):
        return ((x + off // NZ) % nx) * NZ + (z + off % NZ) % NZ

    def rows_of(off):
        return pl.ds(pl.multiple_of(off * chunk, 8), chunk)

    def meta_copy(step):
        off = offset(step)
        to = peer(off)
        return pltpu.make_async_remote_copy(
            src_ref=meta_ref.at[pl.ds(pl.multiple_of(to * 8, 8), 8)],
            dst_ref=meta_recv_ref.at[pl.ds(pl.multiple_of(off * 8, 8), 8)],
            send_sem=meta_send_sem.at[off],
            recv_sem=meta_recv_sem.at[off],
            device_id={"dev": to},
            device_id_type=MESH,
        )

    def data_copy(step):
        off = offset(step)
        return pltpu.make_async_remote_copy(
            src_ref=send_ref.at[rows_of(off)],
            dst_ref=recv_ref.at[rows_of(off)],
            send_sem=send_sem.at[off],
            recv_sem=recv_sem.at[off],
            device_id={"dev": peer(off)},
            device_id_type=MESH,
        )

    def halo_copies(turn, into):
        return [
            pltpu.make_async_remote_copy(
                src_ref=halo_send_ref.at[turn, side],
                dst_ref=into.at[1 - side, pl.ds(0, 3 * halo)],
                send_sem=halo_send_sem.at[turn, side],
                recv_sem=halo_recv_sem.at[turn, side],
                device_id=(prior, after)[side],
                device_id_type=MESH,
            )
            for side in range(2)
        ]

    def pack(off):
        to = peer(off)
        base = pl.multiple_of(off * chunk, 8)
        for k in range(capacity):
            row = source_ref[to, k]
            for p in range(3):
                send_ref[pl.ds(base + (p * capacity + k), 1), :] = tiles_ref[p, pl.ds(row, 1), :]

    barrier = pltpu.get_barrier_semaphore()

    @pl.loop(1, ndev)
    def _(step):
        pl.semaphore_signal(
            barrier, inc=1, device_id={"dev": peer(offset(step))}, device_id_type=MESH
        )

    for other in (prior, after):
        pl.semaphore_signal(barrier, inc=1, device_id=other, device_id_type=MESH)
    pl.semaphore_wait(barrier, ndev + 1)

    @pl.loop(1, ndev)
    def _(step):
        meta_copy(step).start()

    @pl.loop(1, ndev)
    def _(step):
        pack(offset(step))

        @pl.when(step > 1)
        def _():
            data_copy(step - 1).start()

    pack(0)
    data_copy(ndev - 1).start()
    own_rows = pltpu.make_async_copy(send_ref.at[rows_of(0)], recv_ref.at[rows_of(0)], own_sem.at[0])
    own_meta = pltpu.make_async_copy(
        meta_ref.at[pl.ds(pl.multiple_of(me * 8, 8), 8)], meta_recv_ref.at[pl.ds(0, 8)], own_sem.at[1]
    )
    own_meta.start()

    for group in range(5):
        weight = stiffness_ref[group] if group < 3 else (nitsche_ref, coupling_ref)[group - 3][...]
        high, low = halves(weight)
        weights_ref[pl.ds(group * 384, 384), 0:384] = high
        weights_ref[pl.ds(group * 384, 384), 384:768] = low
    own_rows.start()

    own_meta.wait()

    @pl.loop(1, ndev)
    def _(step):
        meta_copy(step).wait()

    blocks = flags_ref.shape[0]
    kind = iota((3 * blocks, LANES), 0) // blocks
    high_of = iota((3 * blocks, LANES), 0) % blocks + 1
    rank = iota((1, LANES), 1)
    flag_bits = flags_ref[...].astype(F32).astype(BF16)
    diagonal = (iota((LANES, LANES), 0) == iota((LANES, LANES), 1)).astype(F32).astype(BF16)
    term = iota((8, LANES), 0)

    def place(off, total):
        base = pl.multiple_of(off * 8, 8)
        meta = meta_recv_ref[pl.ds(base, 8), :]
        high, low, level = meta[0:1].astype(I32), meta[1:2].astype(I32), meta[2:3]
        value = jnp.where(
            kind == 0,
            jnp.full((1, LANES), off, I32).astype(F32),
            jnp.where(kind == 1, rank.astype(F32), level),
        )
        value = jnp.where(high == high_of, value, 0.0)
        column = (low == iota((LANES, LANES), 0)).astype(F32).astype(BF16)
        flag = jnp.where(high == iota((blocks, LANES), 0) + 1, dot(flag_bits, column), 0.0)
        flag = jnp.sum(flag, axis=0, keepdims=True)
        bits = jnp.where(term == 3, flag, (level == term.astype(F32)).astype(F32))
        across = nt_dot(diagonal, bits.astype(BF16))
        arrival_masks_ref[pl.ds(pl.multiple_of(off * capacity, 8), capacity), :] = across[:capacity]
        return total + nt_dot(value.astype(BF16), column)

    total = lax.fori_loop(0, ndev, place, jnp.zeros((3 * blocks, LANES), F32))
    arrival = (total[:blocks] * float(chunk) + total[blocks : 2 * blocks] * 3.0).astype(I32)
    inverse_ref[...] = jnp.clip(arrival, 0, (ndev - 1) * chunk + chunk - 3)
    to_smem = pltpu.make_async_copy(inverse_ref, inverse_smem, own_sem.at[2])
    to_smem.start()
    level = total[2 * blocks :]
    masks_ref[...] = jnp.concatenate(
        [(level == float(index)).astype(F32) for index in range(3)] + [flags_ref[...].astype(F32)],
        axis=0,
    )

    def products(pair):
        offs = [offset(2 * pair + i) for i in range(2)]
        bases = [pl.multiple_of(off * chunk, 8) for off in offs]
        columns = jnp.concatenate(
            [
                arrival_masks_ref[pl.ds(pl.multiple_of(off * capacity, 8), capacity), :]
                for off in offs
            ],
            axis=0,
        )
        masks = [columns[:, l : l + 1].astype(BF16) for l in range(4)]
        high, low = [], []
        for p in range(3):
            h, l = halves(
                jnp.concatenate(
                    [recv_ref[pl.ds(base + p * capacity, capacity), :] for base in bases], axis=0
                )
            )
            high.append(h)
            low.append(l)
        result = dot(jnp.concatenate([h * m for m in masks for h in high], axis=1), weights_ref[0:1536, :])
        own = (
            result[:, :384]
            + result[:, 384:]
            + dot(jnp.concatenate([l * m for m in masks for l in low], axis=1), weights_ref[0:1536, 0:384])
        )
        result = dot(jnp.concatenate(high, axis=1), weights_ref[1536:1920, :])
        near = (
            result[:, :384]
            + result[:, 384:]
            + dot(jnp.concatenate(low, axis=1), weights_ref[1536:1920, 0:384])
        )
        for i, base in enumerate(bases):
            part = slice(i * capacity, (i + 1) * capacity)
            for p in range(3):
                rows = pl.ds(base + p, capacity, stride=3)
                own_ref[rows, :] = own[part, p * LANES : (p + 1) * LANES]
                near_ref[rows, :] = near[part, p * LANES : (p + 1) * LANES]

    own_rows.wait()
    data_copy(1).wait()
    products(0)

    @pl.loop(1, ndev // 2)
    def _(pair):
        data_copy(2 * pair).wait()
        data_copy(2 * pair + 1).wait()
        products(pair)

    def arrival_of(block, lane):
        return jnp.clip(inverse_smem[block, lane], 0, (ndev - 1) * chunk + chunk - 3)

    to_smem.wait()
    for side in range(2):
        for k in range(halo):
            slot = halo_source_ref[side, k]
            row = arrival_of(slot // LANES, slot % LANES)
            halo_send_ref[0, side, pl.ds(3 * k, 3), :] = near_ref[pl.ds(row, 3), :]
        live = iota((3 * halo, LANES), 0) < 3 * count_ref[0, side]
        halo_send_ref[0, side] = jnp.where(live, halo_send_ref[0, side], 0.0)

    def gather(block, carry):
        before, here, row = carry
        base = pl.multiple_of(block * (3 * LANES), 8)
        for k in range(LANES):
            if k < LANES - 1:
                later = arrival_of(block, k + 1)
                ahead = near_ref[pl.ds(later, 3), :]
            else:
                later = arrival_of(jnp.minimum(block + 1, blocks - 1), 0)
                ahead = jnp.where(block < blocks - 1, near_ref[pl.ds(later, 3), :], 0.0)
            sums_ref[pl.ds(base + 3 * k, 3), :] = own_ref[pl.ds(row, 3), :] + (before + ahead)
            before, here, row = here, ahead, later
        return before, here, row

    row = arrival_of(0, 0)
    start = (jnp.zeros((3, LANES), F32), near_ref[pl.ds(row, 3), :], row)
    start = gather(0, start)
    sent = halo_copies(0, arrived_ref)
    for copy in sent:
        copy.start()
    lax.fori_loop(1, blocks, gather, start)
    for p in range(3):
        first_ref[p, 0:PAD, :] = jnp.zeros((PAD, LANES), F32)
        first_ref[p, PAD + count : 2 * PAD + count, :] = jnp.zeros((PAD, LANES), F32)

    for copy in sent:
        copy.wait()
    rows = []
    for side, alive in ((0, has_prev), (1, has_next)):
        row = jnp.concatenate(
            [arrived_ref[side, pl.ds(p, halo, stride=3), :] for p in range(3)], axis=1
        )
        rows.append(jnp.where(alive, row, 0.0))
    high, low = halves(jnp.concatenate(rows, axis=0))
    images_ref[0 : 2 * halo, :] = high
    images_ref[2 * halo : 4 * halo, :] = low

    @pl.loop(0, count // ROWS)
    def _(block):
        added = halo_block(target_ref, images_ref, block)
        base = pl.multiple_of(block * (3 * ROWS), 8)
        rows = pl.ds(pl.multiple_of(block * ROWS, ROWS) + PAD, ROWS)
        for p in range(3):
            first_ref[p, rows, :] = (
                sums_ref[pl.ds(base + p, ROWS, stride=3), :] + added[:, p * LANES : (p + 1) * LANES]
            )

    for side in range(2):
        for k in range(halo):
            row = halo_source_ref[side, k] + PAD
            for p in range(3):
                halo_send_ref[1, side, pl.ds(p * halo + k, 1), :] = first_ref[p, pl.ds(row, 1), :]
        live = iota((halo, LANES), 0) < count_ref[0, side]
        for p in range(3):
            part = pl.ds(p * halo, halo)
            halo_send_ref[1, side, part, :] = jnp.where(live, halo_send_ref[1, side, part, :], 0.0)
    sent = halo_copies(1, arrived2_ref)
    for copy in sent:
        copy.start()
    for copy in sent:
        copy.wait()
    second_halo_ref[...] = arrived2_ref[:, 0 : 3 * halo, :]


def operator_block(field_ref, masks_ref, weights_ref, block):
    base = pl.multiple_of(block * ROWS, ROWS)
    diagonal = (iota((LANES, LANES), 0) == iota((LANES, LANES), 1)).astype(F32).astype(BF16)
    lanes = masks_ref.shape[0] // 4
    columns = jnp.concatenate(
        [
            nt_dot(
                diagonal,
                jnp.concatenate(
                    [masks_ref[pl.ds(l * lanes + block * (ROWS // LANES) + j, 1), :] for l in range(4)],
                    axis=0,
                ).astype(BF16),
            )
            for j in range(ROWS // LANES)
        ],
        axis=0,
    )
    masks = [columns[:, l : l + 1].astype(BF16) for l in range(4)]
    high, low, beside_high, beside_low = [], [], [], []
    for p in range(3):
        wide = field_ref[p, pl.ds(base, ROWS + 2 * PAD), :]
        h, l = halves(wide[PAD : PAD + ROWS])
        high.append(h)
        low.append(l)
        h, l = halves(wide[PAD - 1 : PAD - 1 + ROWS] + wide[PAD + 1 : PAD + 1 + ROWS])
        beside_high.append(h)
        beside_low.append(l)
    left = jnp.concatenate([h * m for m in masks for h in high] + beside_high, axis=1)
    result = dot(left, weights_ref[...])
    left = jnp.concatenate([l * m for m in masks for l in low] + beside_low, axis=1)
    return result[:, :384] + result[:, 384:] + dot(left, weights_ref[:, 0:384])


def halo_images(arrived_ref, weights_ref, images_ref, has_prev, has_next, halo):
    rows = []
    for side, alive in ((0, has_prev), (1, has_next)):
        row = jnp.concatenate(
            [arrived_ref[side, pl.ds(p * halo, halo), :] for p in range(3)], axis=1
        )
        rows.append(jnp.where(alive, row, 0.0))
    high, low = halves(jnp.concatenate(rows, axis=0))
    result = dot(high, weights_ref[1536:1920, :])
    images = result[:, :384] + result[:, 384:] + dot(low, weights_ref[1536:1920, 0:384])
    high, low = halves(images)
    images_ref[0 : 2 * halo, :] = high
    images_ref[2 * halo : 4 * halo, :] = low


def halo_block(target_ref, images_ref, block):
    halo2 = target_ref.shape[1]
    rows = iota((ROWS, halo2), 0) + block * ROWS
    chosen = (rows == target_ref[...]).astype(F32).astype(BF16)
    return dot(jnp.concatenate([chosen, chosen], axis=1), images_ref[...])


def neighbours(groups, ndev):
    group, dev = lax.axis_index("group"), lax.axis_index("dev")
    me = group * ndev + dev
    total = groups * ndev
    after, prior = (me + 1) % total, (me + total - 1) % total
    return me, (prior // ndev, prior % ndev), (after // ndev, after % ndev)


def second_kernel(
    groups,
    ndev,
    field_ref,
    masks_ref,
    weights_ref,
    target_ref,
    arrived_ref,
    first_ref,
    second_ref,
    images_ref,
):
    halo = arrived_ref.shape[1] // 3
    block = pl.program_id(0)

    @pl.when(block == 0)
    def _():
        me, _, _ = neighbours(groups, ndev)
        halo_images(arrived_ref, weights_ref, images_ref, me > 0, me < groups * ndev - 1, halo)

    result = operator_block(field_ref, masks_ref, weights_ref, block)
    result = result + halo_block(target_ref, images_ref, block)
    rows = pl.ds(pl.multiple_of(block * ROWS, ROWS) + PAD, ROWS)
    for p in range(3):
        first_ref[p] = field_ref[p, rows, :]
        second_ref[p] = result[:, p * LANES : (p + 1) * LANES]


def local(
    groups,
    ndev,
    tiles,
    levels,
    new_owner,
    new_slot,
    flags,
    halo_source,
    halo_target,
    halo_count,
    stiffness,
    nitsche,
    coupling,
):
    count = tiles.shape[0]
    halo = halo_source.shape[2]
    blocks = count // LANES
    capacity = count // ndev + count // (4 * ndev)
    planes = jnp.transpose(tiles, (1, 0, 2))
    by_lane = (blocks, LANES)
    shape = jax.ShapeDtypeStruct

    source, meta = pl.pallas_call(
        functools.partial(plan_kernel, ndev),
        out_shape=(shape((ndev, LANES), I32), shape((8 * ndev, LANES), F32)),
        in_specs=[vmem()] * 3,
        out_specs=(vmem(), vmem()),
        name="plan",
    )(new_owner.reshape(by_lane), new_slot.reshape(by_lane), levels.reshape(by_lane))

    arrivals = ndev * 3 * capacity
    targets = halo_target.reshape(1, 2 * halo)
    first, masks, weights, second_halo = pl.pallas_call(
        functools.partial(exchange_kernel, groups, ndev, capacity),
        out_shape=(
            shape((3, count + 2 * PAD, LANES), F32),
            shape((4 * blocks, LANES), F32),
            shape((1920, 768), BF16),
            shape((2, 3 * halo, LANES), F32),
        ),
        in_specs=[smem()] * 3 + [vmem()] * 7,
        out_specs=(vmem(), vmem(), vmem(), vmem()),
        scratch_shapes=[
            pltpu.VMEM((arrivals, LANES), F32),
            pltpu.VMEM((arrivals, LANES), F32),
            pltpu.VMEM((8 * ndev, LANES), F32),
            pltpu.VMEM((ndev * capacity, 8), F32),
            pltpu.VMEM((arrivals + 8, LANES), F32),
            pltpu.VMEM((arrivals + 8, LANES), F32),
            pltpu.VMEM((3 * count + 8, LANES), F32),
            pltpu.VMEM(by_lane, I32),
            pltpu.SMEM(by_lane, I32),
            pltpu.VMEM((2, 2, 3 * halo, LANES), F32),
            pltpu.VMEM((2, 3 * halo + 8, LANES), F32),
            pltpu.VMEM((2, 3 * halo + 8, LANES), F32),
            pltpu.VMEM((4 * halo, 384), BF16),
            pltpu.SemaphoreType.DMA((ndev,)),
            pltpu.SemaphoreType.DMA((ndev,)),
            pltpu.SemaphoreType.DMA((ndev,)),
            pltpu.SemaphoreType.DMA((ndev,)),
            pltpu.SemaphoreType.DMA((3,)),
            pltpu.SemaphoreType.DMA((2, 2)),
            pltpu.SemaphoreType.DMA((2, 2)),
        ],
        compiler_params=pltpu.CompilerParams(
            collective_id=0, has_side_effects=True, vmem_limit_bytes=VMEM_LIMIT
        ),
        name="exchange",
    )(
        source,
        halo_source[0],
        halo_count,
        planes,
        meta,
        flags.reshape(by_lane),
        stiffness,
        nitsche,
        coupling,
        targets,
    )

    block = pl.BlockSpec((3, ROWS, LANES), lambda b: (0, b, 0))
    first, second = pl.pallas_call(
        functools.partial(second_kernel, groups, ndev),
        grid=(count // ROWS,),
        out_shape=(shape(planes.shape, F32), shape(planes.shape, F32)),
        in_specs=[vmem()] * 5,
        out_specs=(block, block),
        scratch_shapes=[pltpu.VMEM((4 * halo, 384), BF16)],
        compiler_params=pltpu.CompilerParams(vmem_limit_bytes=VMEM_LIMIT),
        name="second",
    )(first, masks, weights, targets, second_halo)
    return jnp.transpose(first, (1, 0, 2)), jnp.transpose(second, (1, 0, 2))


def solution(mesh):
    whole = P(("group", "dev"))
    return jax.shard_map(
        functools.partial(local, mesh.shape["group"], mesh.shape["dev"]),
        mesh=mesh,
        in_specs=(
            P(("group", "dev"), None, None),
            whole,
            whole,
            whole,
            whole,
            P(("group", "dev"), None, None),
            P(("group", "dev"), None, None),
            P(("group", "dev"), None),
            P(),
            P(),
            P(),
        ),
        out_specs=(P(("group", "dev"), None, None), P(("group", "dev"), None, None)),
        check_vma=False,
    )
```
